32 devices in a mesh: tm: 4 (over y, x), mom: 8 (over z, core).
Axes of the slice: x: 2, y: 2, z: 4, core: 2. Of those that a mesh axis runs over, the one named last changes fastest.
Arguments:
- g_row: bfloat16 [2, 2, 64, 32, 2048], P(None, None, 'tm', 'mom'), may hold values from -6 to 6
- w_row: bfloat16 [2, 2, 64, 32, 2048], P(None, None, 'tm', 'mom'), may hold values from -6 to 6
- g_col: bfloat16 [2, 2, 64, 32, 2048], P(None, None, 'tm', 'mom'), may hold values from -6 to 6
- rates: float32 [64, 8], P('tm'), may hold values from 0 to 3, as said below
- block_time: int32 [16], replicated, may hold values from 0 to 15, each once
- now: int32 [1], replicated, may hold values from 16 to 63
- rho: float32 [2, 32, 2048], P(None, 'mom'), may hold values from -4 to 4
- slope_one: float32 [2, 32, 2048], P(None, 'mom'), may hold values from -20 to 20
- ham: float32 [2, 32, 2048], P(None, 'mom'), may hold values from -3 to 3
Outputs:
- rho_next: float32 [2, 32, 2048], P(None, 'mom')
- slope_two: float32 [2, 32, 2048], P(None, 'mom')
The draws below stay inside these ranges and needn't reach their ends.
Inputs may be any that keep to these rules, and one draw needn't show every extreme that they name: A permutation: stored block j holds the history times 4 * block_time[j] to 4 * block_time[j] + 3. `now`: the newest time; history times after it carry no weight. Positive rates.
All inputs are finite; a program needn't handle non-finite values.
Results may differ from the reference program's by a relative error of at most 0.0008.
The reference program's roundings to bfloat16 on the way count: a program that leaves them out, or rounds other values in their place, can miss the bound.
Values may be sent and summed in bfloat16 or wider, within the bound.
No kernel may reach another device: no remote copies, remote signals or barrier semaphores. Data moves between devices by JAX's collectives and lax.ppermute only.
A program may use at most 128 MiB of HBM per device.

```python
import math
import jax
import jax.numpy as jnp
from jax import lax

NO = 8
KX = 32
KY = 32
HB = 4
H = 64
NBLK = 16


def draw_rates(key, part):
    keys = jax.random.split(key, 4)
    low = math.log(0.2 / H)
    high = math.log(40.0 / H)
    base = jnp.exp(jax.random.uniform(keys[0], (NO,), minval=low, maxval=high))
    rough = jax.random.uniform(keys[1], (H, NO), minval=0.5, maxval=1.5)
    spots = jax.random.randint(keys[2], (3,), 0, H)
    hits = jnp.sum((jnp.arange(H)[:, None] == spots[None, :]).astype(jnp.float32), axis=1)
    jump = jax.random.uniform(keys[3], (NO,), minval=0.25, maxval=0.6)
    return (base[None, :] * rough + hits[:, None] * jump[None, :]).astype(jnp.float32)


def draw_slope_one(key, part):
    keys = jax.random.split(jax.random.fold_in(key, 17), 1)
    ramp = jnp.arange(KX, dtype=jnp.float32) / (KX - 1)
    scale = jnp.exp(math.log(0.3) + math.log(10.0) * ramp)
    noise = jnp.clip(jax.random.normal(keys[0], (2, KX, KY * NO * NO)), -4.0, 4.0)
    return (noise * scale[None, :, None]).astype(jnp.float32)


def shard_levels(own_key, shape, cuts, least, largest):
    def one(axis_at, shards_of):
        draws = jax.random.uniform(jax.random.fold_in(jax.random.fold_in(own_key, 6), axis_at), (shards_of,), jnp.float32, least / len(cuts), largest / len(cuts))
        return jnp.repeat(jnp.exp(draws), shape[axis_at] // shards_of).reshape((-1,) + (1,) * (len(shape) - axis_at - 1))

    gain = one(*cuts[0])
    for cut in cuts[1:]:
        gain = gain * one(*cut)
    return gain


def gaussian(key, dims, deviation, reach, cuts=(), kind=jnp.bfloat16):
    result = jax.random.normal(key, dims, jnp.float32) * deviation
    if len(cuts) > 0:
        result = shard_levels(key, dims, cuts, -0.22, 0.18) * result
    return jnp.clip(result, min=-reach, max=reach).astype(kind)


def setup_inputs(seed: int = 0) -> dict:
    arg_keys = jax.random.split(jax.random.key(seed), 10)
    g_row = gaussian(arg_keys[0], (2, 2, H, KX, KY * NO * NO), 1.0, 6.0, ((2, 4), (3, 8)))
    w_row = gaussian(arg_keys[1], (2, 2, H, KX, KY * NO * NO), 1.0, 6.0, ((2, 4), (3, 8)))
    g_col = gaussian(arg_keys[2], (2, 2, H, KX, KY * NO * NO), 1.0, 6.0, ((2, 4), (3, 8)))
    rates = draw_rates(jax.random.fold_in(arg_keys[9], 71), 0)
    block_time = jax.random.permutation(arg_keys[4], NBLK).astype(jnp.int32)
    now = jax.random.randint(arg_keys[5], (1,), H // 4, H).astype(jnp.int32)
    rho = gaussian(arg_keys[6], (2, KX, KY * NO * NO), 0.5, 4.0, ((1, 8),), jnp.float32)
    slope_one = draw_slope_one(jax.random.fold_in(arg_keys[9], 71), 0)
    ham = gaussian(arg_keys[8], (2, KX, KY * NO * NO), 0.3, 3.0, ((1, 8),), jnp.float32)
    return dict(g_row=g_row, w_row=w_row, g_col=g_col, rates=rates, block_time=block_time, now=now, rho=rho, slope_one=slope_one, ham=ham)


history_step = 0.01
time_step = 0.1

def dft_table(length, inverse):
    index = jnp.arange(length, dtype=jnp.int32)
    product = index[:, None] * index[None, :] % length
    angle = 2.0 * math.pi / length * product.astype(jnp.float32)
    scale = 1.0 / math.sqrt(length)
    cosine = jnp.cos(angle) * scale
    sine = jnp.sin(angle) * scale
    if inverse:
        sine = -sine
    upper = jnp.stack([cosine, sine], 1)
    lower = jnp.stack([-sine, cosine], 1)
    return jnp.stack([upper, lower], 0).astype(jnp.bfloat16)

def exact_einsum(form, left, right):
    return jnp.einsum(form, left.astype(jnp.float32), right.astype(jnp.float32), precision=lax.Precision.HIGHEST)

def complex_product(left, right):
    real_part = exact_einsum('...ab,...bc->...ac', left[0], right[0]) - exact_einsum('...ab,...bc->...ac', left[1], right[1])
    imag_part = exact_einsum('...ab,...bc->...ac', left[0], right[1]) + exact_einsum('...ab,...bc->...ac', left[1], right[0])
    return jnp.stack([real_part, imag_part], 0)

def section_parts(collide, rho_c, slope_c, ham_c):
    swapped = jnp.swapaxes(collide, -1, -2)
    kernel = jnp.stack([collide[0] + swapped[0], collide[1] - swapped[1]], 0)
    section = rho_c + time_step * slope_c
    commute = complex_product(ham_c, section) - complex_product(section, ham_c)
    slope_two = jnp.stack([commute[1], -commute[0]], 0) + kernel
    joined = slope_c + slope_two
    inner = jnp.sum(slope_c * joined)
    square = jnp.sum(joined * joined)
    return (slope_two, joined, inner, square)

def reference(g_row, w_row, g_col, rates, block_time, now, rho, slope_one, ham):
    now_step = now[0]
    forward_y = dft_table(KY, False)
    forward_x = dft_table(KX, False)
    inverse_x = dft_table(KX, True)
    inverse_y = dft_table(KY, True)
    storage = jnp.arange(H, dtype=jnp.int32)
    times = (block_time[storage // HB] * HB + storage % HB).astype(jnp.int32)
    live = times <= now_step
    masked = jnp.where(live[:, None], rates, jnp.zeros_like(rates))
    in_time = jnp.zeros_like(rates).at[times].set(masked)
    running = jnp.cumsum(in_time, axis=0)
    total = lax.optimization_barrier(jnp.sum(in_time, axis=0))
    decay = jnp.exp(running[times] - total[None, :])
    ends = jnp.logical_or(times == 0, times == now_step)
    weight = jnp.where(live, jnp.where(ends, 0.5, 1.0), 0.0) * history_step
    factor = weight[:, None] * decay
    signs = jnp.array([1.0, -1.0], dtype=rates.dtype)

    def accumulate(step_index, collide):
        green_row = lax.dynamic_index_in_dim(g_row, step_index, 2, keepdims=False)
        screen_row = lax.dynamic_index_in_dim(w_row, step_index, 2, keepdims=False)
        column = lax.dynamic_index_in_dim(g_col, step_index, 2, keepdims=False)
        fields = jnp.concatenate([green_row, screen_row], 0).reshape(4, 2, KX, KY, NO * NO)
        halfway = exact_einsum('oyiq,fixqb->foxyb', forward_y, fields).astype(jnp.bfloat16)
        real_space = exact_einsum('oxip,fipyb->foxyb', forward_x, halfway)
        green = real_space[:2]
        screened = real_space[2:]
        product_real = green[:, 0] * screened[:, 0] - green[:, 1] * screened[:, 1]
        product_imag = green[:, 0] * screened[:, 1] + green[:, 1] * screened[:, 0]
        sigma_real = jnp.stack([-product_imag, product_real], 1).astype(jnp.bfloat16)
        back_x = exact_einsum('oxip,fipyb->foxyb', inverse_x, sigma_real).astype(jnp.bfloat16)
        sigma_k = exact_einsum('oyiq,fixqb->foxyb', inverse_y, back_x).astype(jnp.bfloat16)
        sigma_k = sigma_k.reshape(2, 2, KX, KY, NO, NO)
        column = column.reshape(2, 2, KX, KY, NO, NO)[::-1]
        real_real = exact_einsum('nxyab,nxybc->nxyac', sigma_k[:, 0], column[:, 0])
        imag_imag = exact_einsum('nxyab,nxybc->nxyac', sigma_k[:, 1], column[:, 1])
        real_imag = exact_einsum('nxyab,nxybc->nxyac', sigma_k[:, 0], column[:, 1])
        imag_real = exact_einsum('nxyab,nxybc->nxyac', sigma_k[:, 1], column[:, 0])
        scaled = signs[:, None] * factor[step_index][None, :]
        term = jnp.stack([exact_einsum('na,nxyac->xyac', scaled, real_real - imag_imag), exact_einsum('na,nxyac->xyac', scaled, real_imag + imag_real)], 0)
        return collide + term
    collide = lax.fori_loop(0, H, accumulate, jnp.zeros((2, KX, KY, NO, NO), dtype=rates.dtype))
    shape = collide.shape
    slope_two, joined, inner, square = section_parts(collide, rho.reshape(shape), slope_one.reshape(shape), ham.reshape(shape))
    relax = 4.0 * inner / (square + 1e-06)
    rho_next = rho.reshape(shape) + relax * 0.5 * time_step * joined
    return (rho_next.reshape(rho.shape), slope_two.reshape(rho.shape))
```

```python
import functools
import math

import jax
import jax.numpy as jnp
import numpy as np
from jax import lax
from jax.experimental import pallas as pl
from jax.experimental.pallas import tpu as pltpu
from jax.sharding import PartitionSpec as P

HB = 4
LANES = 128
CHUNKS = 2

history_step = 0.01
time_step = 0.1


def dft_table(length, inverse):
    index = np.arange(length, dtype=np.int32)
    product = index[:, None] * index[None, :] % length
    angle = np.float32(2.0 * math.pi / length) * product.astype(np.float32)
    scale = np.float32(1.0 / math.sqrt(length))
    cosine = (np.cos(angle) * scale).astype(np.float32)
    sine = (np.sin(angle) * scale).astype(np.float32)
    if inverse:
        sine = -sine
    upper = np.stack([cosine, sine], 1)
    lower = np.stack([-sine, cosine], 1)
    return np.stack([upper, lower], 0).astype(jnp.bfloat16).astype(np.float32)


class Plan:
    def __init__(self, mom, tm, g_shape, orbitals):
        self.mom, self.tm = mom, tm
        self.hist, self.kxl = g_shape[2], g_shape[3]
        self.no = orbitals
        self.pairs = orbitals * orbitals
        self.ky = g_shape[4] // self.pairs
        self.kx = self.kxl * mom
        self.yl = self.ky // mom
        self.half = LANES // self.pairs
        self.jy = self.ky // self.half
        self.rows = self.jy * self.kxl
        self.block = self.kxl * 2 * self.yl
        self.full = self.block * mom
        self.lk = self.ky * self.kxl

    def tables(self):
        m, kxl, yl, ky, kx, hf, jy = self.mom, self.kxl, self.yl, self.ky, self.kx, self.half, self.jy
        fy, fx = dft_table(ky, False), dft_table(kx, False)
        ix, iy = dft_table(kx, True), dft_table(ky, True)
        ek, ey = np.eye(kxl, dtype=np.float32), np.eye(yl, dtype=np.float32)
        fy6 = fy.reshape(2, m, yl, 2, jy, hf)
        t1 = np.einsum("odyijh,ab->daoyhijb", fy6, ek).reshape(self.full, -1)
        fx6 = fx.reshape(2, kx, 2, m, kxl)
        t2 = np.einsum("oxidk,ab->oxadkib", fx6, ey).reshape(-1, self.full)
        ix6 = ix.reshape(2, m, kxl, 2, kx)
        t3 = np.einsum("odkix,ab->dkoaixb", ix6, ey).reshape(self.full, -1)
        iy6 = iy.reshape(2, jy, hf, 2, m, yl)
        t4 = np.einsum("ojhidy,ab->daiyohjb", iy6, ek).reshape(self.full, -1)
        return [jnp.asarray(t.astype(jnp.bfloat16)) for t in (t1, t2, t3, t4)]


def dot(a, b):
    return jnp.dot(a, b, preferred_element_type=jnp.float32)


def call(kernel, name, grid=(), **kw):
    flops = kw.pop("flops", 0)
    moved = kw.pop("moved", 0)
    return pl.pallas_call(
        kernel,
        name=name,
        grid=grid,
        cost_estimate=pl.CostEstimate(flops=flops, bytes_accessed=moved, transcendentals=0),
        compiler_params=pltpu.CompilerParams(vmem_limit_bytes=48 * 1024 * 1024),
        **kw,
    )


SMEM_SPEC = pl.BlockSpec(memory_space=pltpu.SMEM)


def halves(first, second, width):
    parts = []
    for h in range(first.shape[-1] // width):
        cut = slice(h * width, (h + 1) * width)
        parts.append(jnp.concatenate([first[:, cut], second[:, cut]], axis=1))
    return jnp.concatenate(parts, axis=0)


def forward_y(plan, me_ref, table_ref, g_ref, w_ref, *out):
    m, blk = plan.mom, plan.block
    outs, table = out[:m], out[m]

    @pl.when(pl.program_id(0) == 0)
    def _():
        for j in range(m):
            src = pl.multiple_of((me_ref[0] ^ j) * blk, blk)
            table[j * blk : (j + 1) * blk, :] = table_ref[pl.ds(src, blk), :]

    count = g_ref.shape[2] // 2

    def tile(t, _):
        gl, sp = t // count, t % count
        sides = []
        for ref in (g_ref, w_ref):
            pair = []
            for p in range(2):
                pair.append(
                    jnp.concatenate([ref[gl, 0, 2 * sp + p], ref[gl, 1, 2 * sp + p]], axis=0)
                )
            sides.append(halves(pair[0], pair[1], plan.pairs))
        y = dot(table[...], jnp.concatenate(sides, axis=1)).astype(jnp.bfloat16)
        for j in range(m):
            outs[j][gl, sp] = y[j * blk : (j + 1) * blk]
        return 0

    lax.fori_loop(0, 2 * count, tile, 0, unroll=2)


def lattice(plan, me_ref, t2_ref, t3_ref, *refs):
    m, blk, full = plan.mom, plan.block, plan.full
    ins, outs, (t2, t3) = refs[:m], refs[m : 2 * m], refs[2 * m :]

    @pl.when(pl.program_id(0) == 0)
    def _():
        me = me_ref[0]
        row = lax.broadcasted_iota(jnp.int32, (full, full), 0)
        col = lax.broadcasted_iota(jnp.int32, (full, full), 1)
        hit = jnp.logical_and((row // blk) == ((col // blk) ^ me), row % blk == col % blk)
        move = jnp.where(hit, 1.0, 0.0).astype(jnp.bfloat16)
        t2[...] = dot(t2_ref[...], move).astype(jnp.bfloat16)
        for j in range(m):
            src = pl.multiple_of((me ^ j) * blk, blk)
            t3[j * blk : (j + 1) * blk, :] = t3_ref[pl.ds(src, blk), :]

    count = ins[0].shape[1]
    half = t2_ref.shape[0] // 2

    def tile(sp, _):
        sides = []
        for gl in range(2):
            x = jnp.concatenate([r[gl, sp] for r in ins], axis=0)
            r = dot(t2[...], x)
            gr, wr = r[:half, :LANES], r[:half, LANES:]
            gi, wi = r[half:, :LANES], r[half:, LANES:]
            real = -(gr * wi + gi * wr)
            imag = gr * wr - gi * wi
            sides.append(jnp.concatenate([real, imag], axis=0).astype(jnp.bfloat16))
        b = dot(t3[...], jnp.concatenate(sides, axis=1)).astype(jnp.bfloat16)
        for gl in range(2):
            for j in range(m):
                outs[j][gl, sp] = b[j * blk : (j + 1) * blk, gl * LANES : (gl + 1) * LANES]
        return 0

    lax.fori_loop(0, count, tile, 0)


def columns(plan, g_ref, o_ref):
    def one(t, _):
        gl, s = t // g_ref.shape[2], t % g_ref.shape[2]
        x = halves(g_ref[gl, 0, s], g_ref[gl, 1, s], plan.pairs)
        o_ref[gl, s] = x.T
        return 0

    lax.fori_loop(0, 2 * g_ref.shape[2], one, 0, unroll=2)


def to_momenta(plan, ref):
    return halves(ref[0], ref[1], plan.pairs).T


def from_momenta(plan, value):
    t = value.T
    n, w = plan.rows, plan.pairs
    return [
        jnp.concatenate([t[h * n : (h + 1) * n, i * w : (i + 1) * w] for h in range(plan.half)], axis=1)
        for i in range(2)
    ]


def prepare(plan, rho_ref, slope_ref, ham_ref, comm_ref, slope_out, left, right):
    no, w = plan.no, plan.pairs
    slope = to_momenta(plan, slope_ref)
    slope_out[...] = slope
    left[...] = to_momenta(plan, ham_ref)
    right[...] = to_momenta(plan, rho_ref) + time_step * slope

    def row(a, _):
        start = pl.multiple_of(a * no, no)
        re = jnp.zeros((no, plan.lk), jnp.float32)
        im = re
        for x, y, sign in ((left, right, 1.0), (right, left, -1.0)):
            for b in range(no):
                xr = x[pl.ds(start + b, 1), :] * sign
                xi = x[pl.ds(w + start + b, 1), :] * sign
                yr = y[b * no : (b + 1) * no, :]
                yi = y[w + b * no : w + (b + 1) * no, :]
                re += xr * yr - xi * yi
                im += xr * yi + xi * yr
        comm_ref[pl.ds(start, no), :] = im
        comm_ref[pl.ds(w + start, no), :] = -re
        return 0

    lax.fori_loop(0, no, row, 0)


def collide(plan, base, me_ref, factor_ref, table_ref, col_ref, *refs):
    m, blk, no, w, lk = plan.mom, plan.block, plan.no, plan.pairs, plan.lk
    first = base == 0
    ins, refs = refs[:m], refs[m:]
    if not first:
        before, refs = refs[0], refs[1:]
    out, table, sig = refs
    for j in range(m):
        src = pl.multiple_of((me_ref[0] ^ j) * blk, blk)
        table[j * blk : (j + 1) * blk, :] = table_ref[pl.ds(src, blk), :]
    count = ins[0].shape[1]

    def step(sp, acc):
        acc = list(acc)
        for gl in range(2):
            x = jnp.concatenate([r[gl, sp] for r in ins], axis=0)
            s = dot(x.T, table[...]).astype(jnp.bfloat16).astype(jnp.float32)
            for p in range(2):
                for a in range(no):
                    fac = factor_ref[base + 2 * sp + p, a] * (1.0 - 2.0 * gl)
                    at = p * w + a * no
                    sig[gl, at : at + no, :] = s[at : at + no, :] * fac
        for gl in range(2):
            for p in range(2):
                c = col_ref[1 - gl, 2 * sp + p].astype(jnp.float32)
                for a in range(no):
                    re, im = acc[a], acc[no + a]
                    for b in range(no):
                        at = p * w + a * no + b
                        sr = sig[gl, at : at + 1, :lk]
                        si = sig[gl, at : at + 1, lk:]
                        cr = c[b * no : (b + 1) * no]
                        ci = c[w + b * no : w + (b + 1) * no]
                        re = re + (sr * cr - si * ci)
                        im = im + (sr * ci + si * cr)
                    acc[a], acc[no + a] = re, im
        return tuple(acc)

    if first:
        start = tuple(jnp.zeros((no, lk), jnp.float32) for _ in range(2 * no))
    else:
        start = tuple(before[i * no : (i + 1) * no, :] for i in range(2 * no))
    acc = lax.fori_loop(0, count, step, start)
    for i in range(2 * no):
        out[i * no : (i + 1) * no, :] = acc[i]


def section(plan, comm_ref, slope_ref, *refs):
    no, w, n = plan.no, plan.pairs, plan.tm
    parts, (slope_two_ref, joined_ref, sums_ref, tot) = refs[:n], refs[n:]
    values = [r[...] for r in parts]
    while len(values) > 1:
        values = [values[i] + values[i + 1] for i in range(0, len(values), 2)]
    tot[...] = values[0]
    out = []
    for i, sign in ((0, 1.0), (1, -1.0)):
        for a in range(no):
            turned = jnp.concatenate(
                [tot[i * w + c * no + a : i * w + c * no + a + 1, :] for c in range(no)], axis=0
            )
            out.append(tot[i * w + a * no : i * w + (a + 1) * no, :] + sign * turned)
    slope_two = comm_ref[...] + jnp.concatenate(out, axis=0)
    slope = slope_ref[...]
    joined = slope + slope_two
    inner = slope * joined
    square = joined * joined
    groups = 2 * w // 8
    sums_ref[0:8, :] = jnp.sum(inner.reshape(groups, 8, plan.lk), axis=0)
    sums_ref[8:16, :] = jnp.sum(square.reshape(groups, 8, plan.lk), axis=0)
    for ref, value in ((slope_two_ref, slope_two), (joined_ref, joined)):
        for i, part in enumerate(from_momenta(plan, value)):
            ref[i] = part


def finish(plan, rho_ref, joined_ref, mine_ref, other_ref, out_ref):
    sums = mine_ref[...] + other_ref[...]
    inner = jnp.sum(sums[0:8], keepdims=True)
    square = jnp.sum(sums[8:16], keepdims=True)
    step = 4.0 * inner / (square + 1e-06) * 0.5 * time_step
    out_ref[...] = rho_ref[...] + step[None] * joined_ref[...]


def xor_permute(x, axis, size, j):
    return lax.ppermute(x, axis, [(i, i ^ j) for i in range(size)])


def local(mom, tm, g_row, w_row, g_col, rates, block_time, now, rho, slope_one, ham):
    no = rates.shape[1]
    plan = Plan(mom, tm, g_row.shape, no)
    hist = plan.hist
    t1, t2, t3, t4 = plan.tables()

    def view(x):
        lead = x.shape[:-2]
        k = len(lead)
        v = x.reshape(lead + (plan.kxl, plan.jy, LANES))
        v = v.transpose(tuple(range(k)) + (k + 1, k, k + 2))
        return v.reshape(lead + (plan.rows, LANES))

    def unview(v):
        lead = v.shape[:-2]
        k = len(lead)
        x = v.reshape(lead + (plan.jy, plan.kxl, LANES))
        x = x.transpose(tuple(range(k)) + (k + 1, k, k + 2))
        return x.reshape(lead + (plan.kxl, plan.jy * LANES))

    me = lax.axis_index("mom").astype(jnp.int32).reshape(1)
    gv, wv, cv = view(g_row), view(w_row), view(g_col)
    rho_v, slope_v, ham_v = view(rho), view(slope_one), view(ham)

    now_step = now[0]
    block_count = hist // HB
    position = lax.axis_index("tm")
    own_blocks = lax.dynamic_slice_in_dim(block_time, position * block_count, block_count)
    times = (own_blocks[:, None] * HB + jnp.arange(HB, dtype=jnp.int32)[None, :]).reshape(hist)
    live = times <= now_step
    masked = jnp.where(live[:, None], rates, 0.0).reshape(block_count, HB, no)
    known = jnp.concatenate(
        [jnp.sum(masked, axis=1), own_blocks.astype(jnp.float32)[:, None]], axis=1
    )
    reach = 1
    while reach < tm:
        known = jnp.concatenate([known, xor_permute(known, "tm", tm, reach)], axis=0)
        reach *= 2
    totals = known[:, :no]
    earlier = (known[None, :, no] < own_blocks.astype(jnp.float32)[:, None]).astype(jnp.float32)
    before = jnp.sum(earlier[:, :, None] * totals[None], axis=1)
    total = jnp.sum(totals, axis=0)
    inside = [masked[:, 0]]
    for i in range(1, HB):
        inside.append(inside[-1] + masked[:, i])
    running = before[:, None, :] + jnp.stack(inside, axis=1)
    decay = jnp.exp(running - total[None, None, :]).reshape(hist, no)
    ends = jnp.logical_or(times == 0, times == now_step)
    weight = jnp.where(live, jnp.where(ends, 0.5, 1.0), 0.0) * history_step
    factor = weight[:, None] * decay

    bf16, f32 = jnp.bfloat16, jnp.float32
    size = hist // CHUNKS
    sps = size // 2
    blk, full, rows, lk, w = plan.block, plan.full, plan.rows, plan.lk, plan.pairs
    vmem = lambda *s: pltpu.VMEM(s, bf16)
    whole = pl.BlockSpec(memory_space=pltpu.VMEM)
    steps = 2 if sps % 2 == 0 else 1
    sb = sps // steps

    def send_first(c):
        spec = pl.BlockSpec(
            (2, 2, 2 * sb, rows, LANES), lambda i: (0, 0, c * steps + i, 0, 0)
        )
        return call(
            functools.partial(forward_y, plan),
            f"forward_y_{c}",
            grid=(steps,),
            in_specs=[SMEM_SPEC, pl.BlockSpec(t1.shape, lambda i: (0, 0)), spec, spec],
            out_specs=[pl.BlockSpec((2, sb, blk, 2 * LANES), lambda i: (0, i, 0, 0))] * mom,
            out_shape=[jax.ShapeDtypeStruct((2, sps, blk, 2 * LANES), bf16)] * mom,
            scratch_shapes=[vmem(*t1.shape)],
            flops=2 * sps * 2 * full * t1.shape[1] * 2 * LANES,
            moved=4 * size * 4 * rows * LANES,
        )(me, t1, gv, wv)

    def middle(c, bufs):
        return call(
            functools.partial(lattice, plan),
            f"lattice_{c}",
            grid=(steps,),
            in_specs=[SMEM_SPEC]
            + [pl.BlockSpec(t.shape, lambda i: (0, 0)) for t in (t2, t3)]
            + [pl.BlockSpec((2, sb, blk, 2 * LANES), lambda i: (0, i, 0, 0))] * mom,
            out_specs=[pl.BlockSpec((2, sb, blk, LANES), lambda i: (0, i, 0, 0))] * mom,
            out_shape=[jax.ShapeDtypeStruct((2, sps, blk, LANES), bf16)] * mom,
            scratch_shapes=[vmem(*t2.shape), vmem(*t3.shape)],
            flops=3 * sps * 2 * full * t2.shape[0] * 2 * LANES,
            moved=6 * size * 2 * rows * LANES,
        )(me, t2, t3, *bufs)

    def last(c, bufs, carry):
        extra = [] if carry is None else [carry]
        return call(
            functools.partial(collide, plan, c * size),
            f"collide_{c}",
            grid=(1,),
            in_specs=[SMEM_SPEC, SMEM_SPEC, pl.BlockSpec(t4.shape, lambda i: (0, 0))]
            + [pl.BlockSpec((2, size, 2 * w, lk), lambda i: (0, c, 0, 0))]
            + [pl.BlockSpec((2, sps, blk, LANES), lambda i: (0, 0, 0, 0))] * mom
            + [pl.BlockSpec((2 * w, lk), lambda i: (0, 0))] * len(extra),
            out_specs=pl.BlockSpec((2 * w, lk), lambda i: (0, 0)),
            out_shape=jax.ShapeDtypeStruct((2 * w, lk), f32),
            scratch_shapes=[vmem(*t4.shape), pltpu.VMEM((2, 2 * w, 2 * lk), f32)],
            flops=2 * sps * 2 * full * t4.shape[0] * LANES,
            moved=6 * size * 2 * rows * LANES,
        )(me, factor, t4, col, *bufs, *extra)

    def exchange(bufs):
        moved = {j: xor_permute(bufs[j], "mom", mom, j) for j in reversed(range(1, mom))}
        return [bufs[0]] + [moved[j] for j in range(1, mom)]

    arrived = [exchange(send_first(c)) for c in range(CHUNKS)]
    col = call(
        functools.partial(columns, plan),
        "columns",
        grid=(1,),
        in_specs=[pl.BlockSpec((2, 2, hist, rows, LANES), lambda i: (0, 0, 0, 0, 0))],
        out_specs=pl.BlockSpec((2, hist, 2 * w, lk), lambda i: (0, 0, 0, 0)),
        out_shape=jax.ShapeDtypeStruct((2, hist, 2 * w, lk), bf16),
        moved=16 * hist * rows * LANES,
    )(cv)
    flat = jax.ShapeDtypeStruct((2 * w, lk), f32)
    comm, slope_k = call(
        functools.partial(prepare, plan),
        "prepare",
        in_specs=[whole] * 3,
        out_specs=[whole] * 2,
        out_shape=[flat] * 2,
        scratch_shapes=[pltpu.VMEM((2 * w, lk), f32)] * 2,
        moved=5 * 4 * 2 * w * lk,
    )(rho_v, slope_v, ham_v)
    back = [exchange(middle(c, arrived[c])) for c in range(CHUNKS)]
    carry = None
    for c in range(CHUNKS):
        carry = last(c, back[c], carry)
    parts = [carry] + [xor_permute(carry, "tm", tm, j) for j in range(1, tm)]
    tiled = jax.ShapeDtypeStruct(rho_v.shape, f32)
    slope_two, joined, sums = call(
        functools.partial(section, plan),
        "section",
        in_specs=[whole] * (2 + tm),
        out_specs=[whole] * 3,
        out_shape=[tiled, tiled, jax.ShapeDtypeStruct((16, lk), f32)],
        scratch_shapes=[pltpu.VMEM((2 * w, lk), f32)],
        moved=8 * 4 * 2 * w * lk,
    )(comm, slope_k, *parts)
    reach = 1
    while reach < mom:
        other = xor_permute(sums, "mom", mom, reach)
        reach *= 2
        if reach < mom:
            sums = sums + other
    rho_next = call(
        functools.partial(finish, plan),
        "finish",
        in_specs=[whole] * 4,
        out_specs=whole,
        out_shape=tiled,
        moved=3 * 4 * 2 * w * lk,
    )(rho_v, joined, sums, other)
    return unview(rho_next), unview(slope_two)


def solution(mesh):
    wide = P(None, None, "tm", "mom", None)
    thin = P(None, "mom", None)
    return jax.shard_map(
        functools.partial(local, mesh.shape["mom"], mesh.shape["tm"]),
        mesh=mesh,
        in_specs=(wide, wide, wide, P("tm", None), P(), P(), thin, thin, thin),
        out_specs=(thin, thin),
        check_vma=False,
    )
```
